32 devices in a mesh: grp: 2 (over x), tile: 8 (over z, y), freq: 2 (over core).
Axes of the slice: x: 2, y: 2, z: 4, core: 2. Of those that a mesh axis runs over, the one named last changes fastest.
Arguments:
- green_recv: bfloat16 [4, 2, 1024, 4096], P(('grp', 'freq'), None, None, 'tile'), parts along dimension 0, may hold values from -2 to 2
- green_shot: bfloat16 [4, 2, 512, 4096], P(('grp', 'freq'), None, None, 'tile'), parts along dimension 0, may hold values from -2.5 to 2.5
- band_mask: int32 [16, 5], P('grp'), parts along dimension 0, may hold values from 0 to 1, as said below
- live_counts: int32 [16], P('grp'), parts along dimension 0, may hold values from 128 to 512, as said below
- freq_bins: int32 [4], P(('grp', 'freq')), parts along dimension 0, may hold values from 256 to 511
Outputs:
- hessian: float32 [8192, 5, 512], P(('grp', 'tile', 'freq')), parts along dimension 0
The draws below stay inside these ranges and needn't reach their ends.
There are 2 independent parts, one for each index of `grp`. The reference program is written for one: setup_inputs(seed, part) draws one part's arguments, and reference() takes and returns one part's arrays. A program takes and returns all parts, laid end to end along the dimension named above; each array names one. Nothing has to cross between parts.
Inputs may be any that keep to these rules, and one draw needn't show every extreme that they name: band_mask[t, 2 + d] equals band_mask[t + d, 2 - d], is 1 at d = 0, is 0 where t + d lies outside the tiles, and some tile has all 5 slots at 1. `live_counts`: some tile has all 512 points live.
All inputs are finite; a program needn't handle non-finite values.
Results may differ from the reference program's by a relative error of at most 0.00065.
Values may be sent and summed in bfloat16 or wider, within the bound.
A program may use at most 64 MiB of HBM per device.

```python
import jax
import jax.numpy as jnp
from jax import lax

RECV = 1024
SHOTS = 512
PTS = 512
REACH = 2
BINS = 512
TILES = 8
FREQS = 2
BAND = 5


def draw_band_mask(key, part):
    first_key, second_key = jax.random.split(jax.random.fold_in(key, 11))
    upper = jax.random.randint(first_key, (TILES, REACH), 0, 2, dtype=jnp.int32)
    center = jax.random.randint(second_key, (), REACH, TILES - REACH, dtype=jnp.int32)
    rows = jnp.arange(TILES, dtype=jnp.int32)[:, None]
    spans = jnp.arange(1, REACH + 1, dtype=jnp.int32)[None, :]
    upper = jnp.where((rows == center) | (rows + spans == center), 1, upper)
    upper = jnp.where(rows + spans < TILES, upper, 0)
    lower_cols = []
    upper_cols = []
    for distance in range(1, REACH + 1):
        column = upper[:, distance - 1]
        upper_cols.append(column)
        lower_cols.append(jnp.concatenate([jnp.zeros((distance,), jnp.int32), column[:TILES - distance]]))
    columns = lower_cols[::-1] + [jnp.ones((TILES,), jnp.int32)] + upper_cols
    return jnp.stack(columns, axis=1).astype(jnp.int32)


def draw_live_counts(key, part):
    first_key, second_key = jax.random.split(jax.random.fold_in(key, 23))
    counts = jax.random.randint(first_key, (TILES,), PTS // 4, PTS + 1, dtype=jnp.int32)
    full_tile = jax.random.randint(second_key, (), 0, TILES, dtype=jnp.int32)
    return jnp.where(jnp.arange(TILES, dtype=jnp.int32) == full_tile, PTS, counts).astype(jnp.int32)


def block_scale(stream_key, extent, cuts, smallest, largest):
    loudness = 1.0
    for position, blocks in cuts:
        heights = jax.random.uniform(jax.random.fold_in(jax.random.fold_in(stream_key, 6), position), (blocks,), jnp.float32, smallest / len(cuts), largest / len(cuts))
        loudness = loudness * jnp.repeat(jnp.exp(heights), extent[position] // blocks).reshape((-1,) + (1,) * (len(extent) - 1 - position))
    return loudness


def centred(stream_key, extent, deviation, reach, cuts=(), kind=jnp.bfloat16):
    drawn = deviation * jax.random.normal(stream_key, extent, jnp.float32)
    if cuts:
        drawn = drawn * block_scale(stream_key, extent, cuts, -0.22, 0.18)
    return jnp.clip(drawn, -reach, reach).astype(kind)


def setup_inputs(seed: int = 0, part: int = 0) -> dict:
    keys = jax.random.split(jax.random.key(seed), 6)
    part_splits = jax.random.split(jax.random.fold_in(keys[5], part), 6)
    green_recv = centred(part_splits[0], (FREQS, 2, RECV, TILES * PTS), 0.15, 2.0, ((0, 2), (3, 8)))
    green_shot = centred(part_splits[1], (FREQS, 2, SHOTS, TILES * PTS), 0.177, 2.5, ((0, 2), (3, 8)))
    band_mask = draw_band_mask(jax.random.fold_in(jax.random.fold_in(keys[5], part), 71), part)
    live_counts = draw_live_counts(jax.random.fold_in(jax.random.fold_in(keys[5], part), 71), part)
    freq_bins = jax.random.randint(part_splits[4], (FREQS,), BINS // 2, BINS).astype(jnp.int32)
    return {"green_recv": green_recv, "green_shot": green_shot, "band_mask": band_mask, "live_counts": live_counts, "freq_bins": freq_bins}


def shift_tiles(field, distance):
    if distance == 0:
        return field
    count = field.shape[-2]
    if distance > 0:
        moved = field[..., distance:, :]
        empty = jnp.zeros(field.shape[:-2] + (distance, field.shape[-1]), field.dtype)
        return jnp.concatenate([moved, empty], axis=-2)
    moved = field[..., :count + distance, :]
    empty = jnp.zeros(field.shape[:-2] + (-distance, field.shape[-1]), field.dtype)
    return jnp.concatenate([empty, moved], axis=-2)


def gram_pair(left_block, right_block):
    product = jnp.einsum("fcrti,fdrtj->tfcidj", left_block, right_block, precision=lax.Precision.HIGHEST)
    real_part = product[:, :, 0, :, 0] + product[:, :, 1, :, 1]
    imag_part = product[:, :, 1, :, 0] - product[:, :, 0, :, 1]
    return real_part, imag_part


def reference(green_recv, green_shot, band_mask, live_counts, freq_bins):
    recv_all = green_recv.astype(jnp.float32).reshape(FREQS, 2, RECV, TILES, PTS)
    shot_all = green_shot.astype(jnp.float32).reshape(FREQS, 2, SHOTS, TILES, PTS)
    weights = (freq_bins.astype(jnp.float32) / BINS) ** 4
    live_mask = (jnp.arange(PTS, dtype=jnp.int32)[None, :] < live_counts[:, None]).astype(jnp.float32)
    blocks = []
    for offset in range(-REACH, REACH + 1):
        recv_real, recv_imag = gram_pair(recv_all, shift_tiles(recv_all, offset))
        shot_real, shot_imag = gram_pair(shot_all, shift_tiles(shot_all, offset))
        summed = jnp.einsum("f,tfij->tij", weights, recv_real * shot_real - recv_imag * shot_imag,
                            precision=lax.Precision.HIGHEST)
        far_live = shift_tiles(live_mask, offset)
        active = band_mask[:, REACH + offset].astype(jnp.float32)
        blocks.append(summed * active[:, None, None] * live_mask[:, :, None] * far_live[:, None, :])
    hessian = jnp.stack(blocks, axis=2)
    return hessian.reshape(TILES * PTS, BAND, PTS)
```

```python
import functools

import jax
import jax.numpy as jnp
from jax import lax
from jax.experimental import pallas as pl
from jax.experimental.pallas import tpu as pltpu
from jax.sharding import PartitionSpec as P

BINS = 512
MESH = pl.DeviceIdType.MESH
PAIRS = ((0, 1), (0, 2), (1, 2))
ROW = {1: 0, 2: 1, -1: 2, -2: 3}


def band_kernel(tiles, radius, recv_ref, shot_ref, band_ref, live_ref, bins_ref, out_ref,
                far_r, far_s, left_r, left_s, local, self_local, self_out, self_in, outbox, inbox,
                own_sem, data_send, data_recv, res_send, res_recv, self_send, self_recv):
    t = lax.axis_index("tile")
    f = lax.axis_index("freq")
    depth_r, points = recv_ref.shape
    depth_s = shot_ref.shape[0]
    half = points // 2
    step = 1 - 2 * f
    r = f * (tiles - 1) + step * t
    heavy = lax.rem(r, 2) == 0
    has_far = r + 2 < tiles
    weight_root = bins_ref[0].astype(jnp.float32) / BINS
    weight = (weight_root * weight_root) * (weight_root * weight_root)

    def columns(j):
        return pl.ds(pl.multiple_of(j * half, half), half)

    def own_copy(which, j):
        src, dst = ((recv_ref, far_r), (shot_ref, far_s))[which]
        return pltpu.make_async_copy(src.at[:, columns(j)], dst.at[0, j], own_sem.at[which, j])

    def data_copy(which, j, distance):
        src, dst = ((recv_ref, far_r), (shot_ref, far_s))[which]
        return pltpu.make_async_remote_copy(
            src_ref=src.at[:, columns(j)], dst_ref=dst.at[distance, j],
            send_sem=data_send.at[which, j, distance - 1], recv_sem=data_recv.at[which, j, distance - 1],
            device_id={"tile": t - step * distance}, device_id_type=MESH)

    for j in range(2):
        for which in range(2):
            own_copy(which, j).start()

    barrier = pltpu.get_barrier_semaphore()
    for distance in range(-2, 3):
        near = t + distance
        for turn in range(2):
            if distance == 0 and turn == 0:
                continue
            other = f if turn == 0 else 1 - f

            @pl.when((near >= 0) & (near < tiles))
            def _():
                pl.semaphore_signal(barrier, inc=1, device_id={"tile": near, "freq": other}, device_id_type=MESH)
    reached = jnp.minimum(t, 2) + jnp.minimum(tiles - 1 - t, 2)
    pl.semaphore_wait(barrier, 2 * reached + 1)

    for j in range(2):
        for which in range(2):
            @pl.when(jnp.logical_not(heavy))
            def _():
                data_copy(which, j, 1).start()

            @pl.when(r >= 2)
            def _():
                data_copy(which, j, 2).start()

    def build_left(slot, j):
        for src, dst, depth in ((far_r, left_r, depth_r // 2), (far_s, left_s, depth_s // 2)):
            part = min(depth, 512)

            @pl.loop(0, depth // part)
            def _(k):
                lo = pl.multiple_of(k * part, part)
                hi = pl.multiple_of(depth + k * part, part)
                re = src[slot, j, pl.ds(lo, part), :].T
                im = src[slot, j, pl.ds(hi, part), :].T
                dst[slot, j, 0:half, pl.ds(lo, part)] = re
                dst[slot, j, 0:half, pl.ds(hi, part)] = im
                dst[slot, j, half:points, pl.ds(lo, part)] = im
                dst[slot, j, half:points, pl.ds(hi, part)] = -re

    def block(slot, h, far, j):
        rr = jnp.dot(left_r[slot, h], far_r[far, j], preferred_element_type=jnp.float32)
        ss = jnp.dot(left_s[slot, h], far_s[far, j], preferred_element_type=jnp.float32)
        return (rr[:half] * ss[:half] - rr[half:] * ss[half:]) * weight

    def far_from(h):
        return jnp.where(h == f, 0, 1)

    def plain_send(k, h, j):
        first, second = PAIRS[k]
        return pltpu.make_async_remote_copy(
            src_ref=outbox.at[k, h, j, 0], dst_ref=inbox.at[far_from(h), ROW[second - first], j],
            send_sem=res_send.at[k, h, j, 0], recv_sem=res_recv.at[far_from(h), ROW[second - first], j],
            device_id={"tile": t + step * first, "freq": h}, device_id_type=MESH)

    def turned_send(k, h, j):
        first, second = PAIRS[k]
        return pltpu.make_async_remote_copy(
            src_ref=outbox.at[k, h, j, 1], dst_ref=inbox.at[far_from(j), ROW[first - second], h],
            send_sem=res_send.at[k, h, j, 1], recv_sem=res_recv.at[far_from(j), ROW[first - second], h],
            device_id={"tile": t + step * second, "freq": j}, device_id_type=MESH)

    def unit(k, h, j):
        first, second = PAIRS[k]
        value = block(first, h, second, j)
        outbox[k, h, j, 1] = value.T.astype(jnp.bfloat16)
        turned_send(k, h, j).start()
        if first == 0:
            @pl.when(h == f)
            def _():
                local[second - 1, j] = value

            @pl.when(h != f)
            def _():
                outbox[k, h, j, 0] = value.astype(jnp.bfloat16)
                plain_send(k, h, j).start()
        else:
            outbox[k, h, j, 0] = value.astype(jnp.bfloat16)
            plain_send(k, h, j).start()

    def self_copy(j):
        return pltpu.make_async_remote_copy(
            src_ref=self_out.at[j], dst_ref=self_in.at[j], send_sem=self_send.at[j], recv_sem=self_recv.at[j],
            device_id={"freq": 1 - f}, device_id_type=MESH)

    for j in range(2):
        for which in range(2):
            own_copy(which, j).wait()

    @pl.loop(0, 2)
    def _(j):
        build_left(0, j)

    @pl.loop(0, 2)
    def _(j):
        self_local[j] = block(0, f, 0, j)

    @pl.loop(0, 2)
    def _(j):
        self_out[j] = block(0, 1 - f, 0, j)
        self_copy(j).start()

    @pl.loop(0, 2)
    def _(j):
        @pl.when(heavy)
        def _():
            for which in range(2):
                data_copy(which, j, 1).wait_recv()

            @pl.loop(0, 2)
            def _(h):
                unit(0, h, j)

            build_left(1, j)

        @pl.when(has_far)
        def _():
            for which in range(2):
                data_copy(which, j, 2).wait_recv()

            @pl.loop(0, 2)
            def _(h):
                unit(1, h, j)

        @pl.when(heavy & has_far)
        def _():
            @pl.loop(0, 2 * j + 1)
            def _(i):
                unit(2, jnp.minimum(i, j), j - jnp.maximum(i - j, 0))

    rows = lax.broadcasted_iota(jnp.int32, (half, half), 0) + f * half
    cols = lax.broadcasted_iota(jnp.int32, (half, half), 1)
    row_live = rows < live_ref[t]

    @pl.loop(0, 2)
    def _(j):
        self_copy(j).wait_recv()
        keep = row_live & (cols + j * half < live_ref[t]) & (band_ref[t, radius] > 0)
        out_ref[radius, :, columns(j)] = jnp.where(keep, self_local[j] + self_in[j], 0.0)

    def wait_inbox(origin, row, j):
        pltpu.make_async_remote_copy(
            src_ref=outbox.at[0, 0, 0, 0], dst_ref=inbox.at[origin, row, j],
            send_sem=res_send.at[0, 0, 0, 0], recv_sem=res_recv.at[origin, row, j],
            device_id={"freq": 1 - f}, device_id_type=MESH).wait_recv()

    for delta in (1, -1, -2, 2):
        near = t + step * delta
        slot = radius + step * delta
        exists = (r + delta >= 0) & (r + delta < tiles)

        def emit(j, own, near=near, slot=slot, delta=delta):
            wait_inbox(1, ROW[-delta], j)
            total = own + inbox[1, ROW[-delta], j].astype(jnp.float32)
            keep = row_live & (cols + j * half < live_ref[near]) & (band_ref[t, slot] > 0)
            out_ref[slot, :, columns(j)] = jnp.where(keep, total, 0.0)

        def from_inbox(delta=delta, emit=emit):
            @pl.loop(0, 2)
            def _(j):
                wait_inbox(0, ROW[delta], j)
                emit(j, inbox[0, ROW[delta], j].astype(jnp.float32))

        def from_local(delta=delta, emit=emit):
            @pl.loop(0, 2)
            def _(j):
                emit(j, local[delta - 1, j])

        if delta == 2:
            pl.when(exists)(from_local)
        elif delta == 1:
            pl.when(exists & heavy)(from_local)
            pl.when(exists & jnp.logical_not(heavy))(from_inbox)
        else:
            pl.when(exists)(from_inbox)

        @pl.when(jnp.logical_not(exists))
        def _():
            out_ref[slot] = jnp.zeros((half, points), jnp.float32)

    for j in range(2):
        self_copy(j).wait_send()
        for which in range(2):
            @pl.when(jnp.logical_not(heavy))
            def _():
                data_copy(which, j, 1).wait_send()

            @pl.when(r >= 2)
            def _():
                data_copy(which, j, 2).wait_send()

    for k, (first, second) in enumerate(PAIRS):
        made = heavy if second == 1 else (has_far if first == 0 else heavy & has_far)

        @pl.when(made)
        def _():
            @pl.loop(0, 2)
            def _(h):
                for j in range(2):
                    turned_send(k, h, j).wait_send()
                    if first == 0:
                        @pl.when(h != f)
                        def _():
                            plain_send(k, h, j).wait_send()
                    else:
                        plain_send(k, h, j).wait_send()


def per_device(green_recv, green_shot, band_mask, live_counts, freq_bins):
    tiles = lax.axis_size("tile")
    points = green_recv.shape[3]
    slots = band_mask.shape[1]
    half = points // 2
    depth_r = 2 * green_recv.shape[2]
    depth_s = 2 * green_shot.shape[2]
    bf16, f32 = jnp.bfloat16, jnp.float32
    dma = pltpu.SemaphoreType.DMA
    smem = pl.BlockSpec(memory_space=pltpu.SMEM)
    band = pl.pallas_call(
        functools.partial(band_kernel, tiles, slots // 2),
        out_shape=jax.ShapeDtypeStruct((slots, half, points), f32),
        in_specs=[pl.BlockSpec(memory_space=pl.ANY)] * 2 + [smem] * 3,
        out_specs=pl.BlockSpec(memory_space=pltpu.VMEM),
        scratch_shapes=[
            pltpu.VMEM((3, 2, depth_r, half), bf16),
            pltpu.VMEM((3, 2, depth_s, half), bf16),
            pltpu.VMEM((2, 2, points, depth_r), bf16),
            pltpu.VMEM((2, 2, points, depth_s), bf16),
            pltpu.VMEM((2, 2, half, half), f32),
            pltpu.VMEM((2, half, half), f32),
            pltpu.VMEM((2, half, half), f32),
            pltpu.VMEM((2, half, half), f32),
            pltpu.VMEM((3, 2, 2, 2, half, half), bf16),
            pltpu.VMEM((2, 4, 2, half, half), bf16),
            dma((2, 2)),
            dma((2, 2, 2)),
            dma((2, 2, 2)),
            dma((3, 2, 2, 2)),
            dma((2, 4, 2)),
            dma((2,)),
            dma((2,)),
        ],
        compiler_params=pltpu.CompilerParams(
            collective_id=0, has_side_effects=True, vmem_limit_bytes=60 * 1024 * 1024),
    )(green_recv.reshape(depth_r, points), green_shot.reshape(depth_s, points), band_mask, live_counts, freq_bins)
    return jnp.transpose(band, (1, 0, 2))


def solution(mesh):
    return jax.shard_map(
        per_device,
        mesh=mesh,
        in_specs=(
            P(("grp", "freq"), None, None, "tile"),
            P(("grp", "freq"), None, None, "tile"),
            P("grp", None),
            P("grp"),
            P(("grp", "freq")),
        ),
        out_specs=P(("grp", "tile", "freq"), None, None),
        check_vma=False,
    )
```

```python
import functools

import jax
import jax.numpy as jnp
from jax import lax
from jax.experimental import pallas as pl
from jax.experimental.pallas import tpu as pltpu
from jax.sharding import PartitionSpec as P

BINS = 512
MESH = pl.DeviceIdType.MESH
PAIR = {(1, 0): 0, (2, 0): 1, (2, 1): 2, (1, 2): 2}
ROW = {1: 0, 2: 1, -1: 2, -2: 3}


def band_kernel(tiles, radius, recv_ref, shot_ref, band_ref, live_ref, bins_ref, out_ref,
                far_r, far_s, left_r, left_s, local, self_local, self_out, self_in, outbox, turned, inbox,
                own_sem, data_send, data_recv, res_send, res_recv, self_send, self_recv):
    t = lax.axis_index("tile")
    f = lax.axis_index("freq")
    depth_r, points = recv_ref.shape
    depth_s = shot_ref.shape[0]
    half = points // 2
    part = half // 2
    step = 1 - 2 * f
    r = f * (tiles - 1) + step * t
    heavy = lax.rem(r, 2) == 0
    has_far = r + 2 < tiles
    weight_root = bins_ref[0].astype(jnp.float32) / BINS
    weight = (weight_root * weight_root) * (weight_root * weight_root)

    def columns(j):
        return pl.ds(pl.multiple_of(j * half, half), half)

    def parts(i):
        return pl.ds(pl.multiple_of(i * part, part), part)

    def own_copy(which, j):
        src, dst = ((recv_ref, far_r), (shot_ref, far_s))[which]
        return pltpu.make_async_copy(src.at[:, columns(j)], dst.at[0, j], own_sem.at[which, j])

    def data_copy(which, i, distance):
        src, dst = ((recv_ref, far_r), (shot_ref, far_s))[which]
        return pltpu.make_async_remote_copy(
            src_ref=src.at[:, parts(i)], dst_ref=dst.at[distance, i // 2, :, parts(i % 2)],
            send_sem=data_send.at[which, i, distance - 1], recv_sem=data_recv.at[which, i, distance - 1],
            device_id={"tile": t - step * distance}, device_id_type=MESH)

    for j in range(2):
        for which in range(2):
            own_copy(which, j).start()

    barrier = pltpu.get_barrier_semaphore()
    for distance in range(-2, 3):
        near = t + distance
        for turn in range(2):
            if distance == 0 and turn == 0:
                continue
            other = f if turn == 0 else 1 - f

            @pl.when((near >= 0) & (near < tiles))
            def _():
                pl.semaphore_signal(barrier, inc=1, device_id={"tile": near, "freq": other}, device_id_type=MESH)
    reached = jnp.minimum(t, 2) + jnp.minimum(tiles - 1 - t, 2)
    pl.semaphore_wait(barrier, 2 * reached + 1)

    for i in range(4):
        for which in range(2):
            @pl.when(jnp.logical_not(heavy))
            def _():
                data_copy(which, i, 1).start()

            @pl.when(r >= 2)
            def _():
                data_copy(which, i, 2).start()

    def build_left(slot, i):
        for src, dst, depth in ((far_r, left_r, depth_r // 2), (far_s, left_s, depth_s // 2)):
            re = src[slot, i // 2, 0:depth, parts(i % 2)].T
            im = src[slot, i // 2, depth:2 * depth, parts(i % 2)].T
            dst[slot, i, 0:part, 0:depth] = re
            dst[slot, i, 0:part, depth:2 * depth] = im
            dst[slot, i, part:half, 0:depth] = im
            dst[slot, i, part:half, depth:2 * depth] = -re

    def block(left, i, right, h):
        rr = jnp.dot(left_r[left, i], far_r[right, h], preferred_element_type=jnp.float32)
        ss = jnp.dot(left_s[left, i], far_s[right, h], preferred_element_type=jnp.float32)
        return (rr[:part] * ss[:part] - rr[part:] * ss[part:]) * weight

    def origin_at(h):
        return jnp.where(h == f, 0, 1)

    def plain_send(left, i, right, h, n):
        k, origin, row = PAIR[left, right], origin_at(i // 2), ROW[right - left]
        return pltpu.make_async_remote_copy(
            src_ref=outbox.at[k, n], dst_ref=inbox.at[origin, row, parts(i % 2), columns(h)],
            send_sem=res_send.at[k, 0], recv_sem=res_recv.at[origin, row],
            device_id={"tile": t + step * left, "freq": i // 2}, device_id_type=MESH)

    def turned_send(left, i, right, h, n):
        k, origin, row = PAIR[left, right], origin_at(h), ROW[left - right]
        return pltpu.make_async_remote_copy(
            src_ref=turned.at[k, n], dst_ref=inbox.at[origin, row, :, parts(i)],
            send_sem=res_send.at[k, 1], recv_sem=res_recv.at[origin, row],
            device_id={"tile": t + step * right, "freq": h}, device_id_type=MESH)

    def unit(left, i, right, h, n):
        k = PAIR[left, right]
        value = block(left, i, right, h)
        outbox[k, n] = value.astype(jnp.bfloat16)
        plain_send(left, i, right, h, n).start()
        if right == 0:
            @pl.when(h == f)
            def _():
                local[left - 1, :, parts(i)] = value.T

            @pl.when(h != f)
            def _():
                turned[k, n] = value.T.astype(jnp.bfloat16)
                turned_send(left, i, right, h, n).start()
        else:
            turned[k, n] = value.T.astype(jnp.bfloat16)
            turned_send(left, i, right, h, n).start()

    def self_copy():
        return pltpu.make_async_remote_copy(
            src_ref=self_out, dst_ref=self_in, send_sem=self_send, recv_sem=self_recv,
            device_id={"freq": 1 - f}, device_id_type=MESH)

    for j in range(2):
        for which in range(2):
            own_copy(which, j).wait()

    @pl.loop(0, 4)
    def _(i):
        build_left(0, i)

    for target, dest in ((1 - f, self_out), (f, self_local)):
        @pl.loop(0, 4)
        def _(m):
            dest[parts(m // 2), columns(m % 2)] = block(0, 2 * target + m // 2, 0, m % 2)

        if dest is self_out:
            self_copy().start()

    @pl.loop(0, 4)
    def _(i):
        @pl.when(heavy)
        def _():
            for which in range(2):
                data_copy(which, i, 1).wait_recv()
            build_left(1, i)

            @pl.loop(0, 2)
            def _(h):
                unit(1, i, 0, h, 2 * i + h)

        @pl.when(has_far)
        def _():
            for which in range(2):
                data_copy(which, i, 2).wait_recv()
            build_left(2, i)

            @pl.loop(0, 2)
            def _(h):
                unit(2, i, 0, h, 2 * i + h)

        @pl.when(heavy & has_far)
        def _():
            @pl.loop(0, jnp.where(i == 1, 2, jnp.where(i == 0, 0, 2 * i - 3)))
            def _(m):
                n = jnp.where(i == 1, 2 * m, i + 2 + m)
                unit(2, n // 2, 1, n % 2, n)

            @pl.when(i >= 2)
            def _():
                unit(1, i, 2, 0, 2 * i - 3)

    rows = lax.broadcasted_iota(jnp.int32, (half, half), 0) + f * half
    cols = lax.broadcasted_iota(jnp.int32, (half, half), 1)
    row_live = rows < live_ref[t]

    self_copy().wait_recv()

    @pl.loop(0, 2)
    def _(j):
        keep = row_live & (cols + j * half < live_ref[t]) & (band_ref[t, radius] > 0)
        out_ref[radius, :, columns(j)] = jnp.where(keep, self_local[:, columns(j)] + self_in[:, columns(j)], 0.0)

    def wait_inbox(origin, row):
        pltpu.make_async_remote_copy(
            src_ref=inbox.at[origin, row], dst_ref=inbox.at[origin, row],
            send_sem=res_send.at[0, 0], recv_sem=res_recv.at[origin, row],
            device_id={"freq": 1 - f}, device_id_type=MESH).wait_recv()

    for delta in (1, -1, -2, 2):
        near = t + step * delta
        slot = radius + step * delta
        exists = (r + delta >= 0) & (r + delta < tiles)

        def emit(j, own, near=near, slot=slot, delta=delta):
            total = own + inbox[1, ROW[-delta], :, columns(j)].astype(jnp.float32)
            keep = row_live & (cols + j * half < live_ref[near]) & (band_ref[t, slot] > 0)
            out_ref[slot, :, columns(j)] = jnp.where(keep, total, 0.0)

        def from_inbox(delta=delta, emit=emit):
            wait_inbox(0, ROW[delta])
            wait_inbox(1, ROW[-delta])

            @pl.loop(0, 2)
            def _(j):
                emit(j, inbox[0, ROW[delta], :, columns(j)].astype(jnp.float32))

        def from_local(delta=delta, emit=emit):
            wait_inbox(1, ROW[-delta])

            @pl.loop(0, 2)
            def _(j):
                emit(j, local[delta - 1, :, columns(j)])

        if delta == 2:
            pl.when(exists)(from_local)
        elif delta == 1:
            pl.when(exists & heavy)(from_local)
            pl.when(exists & jnp.logical_not(heavy))(from_inbox)
        else:
            pl.when(exists)(from_inbox)

        @pl.when(jnp.logical_not(exists))
        def _():
            out_ref[slot] = jnp.zeros((half, points), jnp.float32)

    self_copy().wait_send()
    for i in range(4):
        for which in range(2):
            @pl.when(jnp.logical_not(heavy))
            def _():
                data_copy(which, i, 1).wait_send()

            @pl.when(r >= 2)
            def _():
                data_copy(which, i, 2).wait_send()

    def wait_sent(box, sem):
        pltpu.make_async_remote_copy(
            src_ref=box, dst_ref=box, send_sem=sem, recv_sem=res_recv.at[0, 0],
            device_id={"freq": 1 - f}, device_id_type=MESH).wait_send()

    for k, made in enumerate((heavy, has_far, heavy & has_far)):
        @pl.when(made)
        def _():
            wait_sent(outbox.at[k], res_send.at[k, 0])
            wait_sent(turned.at[k] if k == 2 else turned.at[k, 0:4], res_send.at[k, 1])


def per_device(green_recv, green_shot, band_mask, live_counts, freq_bins):
    tiles = lax.axis_size("tile")
    points = green_recv.shape[3]
    slots = band_mask.shape[1]
    half = points // 2
    depth_r = 2 * green_recv.shape[2]
    depth_s = 2 * green_shot.shape[2]
    bf16, f32 = jnp.bfloat16, jnp.float32
    dma = pltpu.SemaphoreType.DMA
    smem = pl.BlockSpec(memory_space=pltpu.SMEM)
    band = pl.pallas_call(
        functools.partial(band_kernel, tiles, slots // 2),
        out_shape=jax.ShapeDtypeStruct((slots, half, points), f32),
        in_specs=[pl.BlockSpec(memory_space=pl.ANY)] * 2 + [smem] * 3,
        out_specs=pl.BlockSpec(memory_space=pltpu.VMEM),
        scratch_shapes=[
            pltpu.VMEM((3, 2, depth_r, half), bf16),
            pltpu.VMEM((3, 2, depth_s, half), bf16),
            pltpu.VMEM((3, 4, half, depth_r), bf16),
            pltpu.VMEM((3, 4, half, depth_s), bf16),
            pltpu.VMEM((2, half, points), f32),
            pltpu.VMEM((half, points), f32),
            pltpu.VMEM((half, points), f32),
            pltpu.VMEM((half, points), f32),
            pltpu.VMEM((3, 8, half // 2, half), bf16),
            pltpu.VMEM((3, 8, half, half // 2), bf16),
            pltpu.VMEM((2, 4, half, points), bf16),
            dma((2, 2)),
            dma((2, 4, 2)),
            dma((2, 4, 2)),
            dma((3, 2)),
            dma((2, 4)),
            dma,
            dma,
        ],
        compiler_params=pltpu.CompilerParams(
            collective_id=0, has_side_effects=True, vmem_limit_bytes=60 * 1024 * 1024),
    )(green_recv.reshape(depth_r, points), green_shot.reshape(depth_s, points), band_mask, live_counts, freq_bins)
    return jnp.transpose(band, (1, 0, 2))


def solution(mesh):
    return jax.shard_map(
        per_device,
        mesh=mesh,
        in_specs=(
            P(("grp", "freq"), None, None, "tile"),
            P(("grp", "freq"), None, None, "tile"),
            P("grp", None),
            P("grp"),
            P(("grp", "freq")),
        ),
        out_specs=P(("grp", "tile", "freq"), None, None),
        check_vma=False,
    )
```

```python
import functools

import jax
import jax.numpy as jnp
from jax import lax
from jax.experimental import pallas as pl
from jax.experimental.pallas import tpu as pltpu
from jax.sharding import PartitionSpec as P

BINS = 512
VMEM_MIB = 60
MESH = pl.DeviceIdType.MESH
PAIR = {(1, 0): 0, (2, 0): 1, (2, 1): 2, (1, 2): 2}
ROW = {1: 0, 2: 1, -1: 2, -2: 3}


def place(tiles):
    t = lax.axis_index("tile")
    f = lax.axis_index("freq")
    step = 1 - 2 * f
    r = f * (tiles - 1) + step * t
    return t, f, step, r, lax.rem(r, 2) == 0


def band_kernel(tiles, recv_ref, shot_ref, bins_ref, inbox, kept,
                far_r, far_s, left_r, left_s, own, self_out, self_in, outbox, turned,
                own_sem, kept_sem, data_send, data_recv, res_send, res_recv, self_send, self_recv):
    t, f, step, r, heavy = place(tiles)
    depth_r, points = recv_ref.shape
    depth_s = shot_ref.shape[0]
    half = points // 2
    part = half // 2
    has_far = r + 2 < tiles
    weight_root = bins_ref[0].astype(jnp.float32) / BINS
    weight = (weight_root * weight_root) * (weight_root * weight_root)

    def columns(j):
        return pl.ds(pl.multiple_of(j * half, half), half)

    def parts(i):
        return pl.ds(pl.multiple_of(i * part, part), part)

    def own_copy(which, j):
        src, dst = ((recv_ref, far_r), (shot_ref, far_s))[which]
        return pltpu.make_async_copy(src.at[:, columns(j)], dst.at[0, j], own_sem.at[which, j])

    def data_copy(which, i, distance):
        src, dst = ((recv_ref, far_r), (shot_ref, far_s))[which]
        return pltpu.make_async_remote_copy(
            src_ref=src.at[:, parts(i)], dst_ref=dst.at[distance, i // 2, :, parts(i % 2)],
            send_sem=data_send.at[which, i, distance - 1], recv_sem=data_recv.at[which, i, distance - 1],
            device_id={"tile": t - step * distance}, device_id_type=MESH)

    barrier = pltpu.get_barrier_semaphore()
    for distance in range(-2, 3):
        near = t + distance
        for turn in range(2):
            if distance == 0 and turn == 0:
                continue
            other = f if turn == 0 else 1 - f

            @pl.when((near >= 0) & (near < tiles))
            def _():
                pl.semaphore_signal(barrier, inc=1, device_id={"tile": near, "freq": other}, device_id_type=MESH)
    reached = jnp.minimum(t, 2) + jnp.minimum(tiles - 1 - t, 2)
    for j in range(2):
        for which in range(2):
            own_copy(which, j).start()

    pl.semaphore_wait(barrier, 2 * reached + 1)

    for i in range(4):
        for which in range(2):
            @pl.when(jnp.logical_not(heavy))
            def _():
                data_copy(which, i, 1).start()

            @pl.when(r >= 2)
            def _():
                data_copy(which, i, 2).start()

    def build_left(slot, i):
        for src, dst, depth in ((far_r, left_r, depth_r // 2), (far_s, left_s, depth_s // 2)):
            re = src[slot, i // 2, 0:depth, parts(i % 2)].T
            im = src[slot, i // 2, depth:2 * depth, parts(i % 2)].T
            dst[slot, i, 0:part, 0:depth] = re
            dst[slot, i, 0:part, depth:2 * depth] = im
            dst[slot, i, part:half, 0:depth] = im
            dst[slot, i, part:half, depth:2 * depth] = -re

    def block(left, i, right, h):
        rr = jnp.dot(left_r[left, i], far_r[right, h], preferred_element_type=jnp.float32)
        ss = jnp.dot(left_s[left, i], far_s[right, h], preferred_element_type=jnp.float32)
        return (rr[:part] * ss[:part] - rr[part:] * ss[part:]) * weight

    def origin_at(h):
        return jnp.where(h == f, 0, 1)

    def plain_send(left, i, right, h, n):
        k, origin, row = PAIR[left, right], origin_at(i // 2), ROW[right - left]
        return pltpu.make_async_remote_copy(
            src_ref=outbox.at[k, n], dst_ref=inbox.at[origin, row, parts(i % 2), columns(h)],
            send_sem=res_send.at[k, 0], recv_sem=res_recv.at[origin, row],
            device_id={"tile": t + step * left, "freq": i // 2}, device_id_type=MESH)

    def turned_send(left, i, right, h, n):
        k, origin, row = PAIR[left, right], origin_at(h), ROW[left - right]
        return pltpu.make_async_remote_copy(
            src_ref=turned.at[k, n], dst_ref=inbox.at[origin, row, :, parts(i)],
            send_sem=res_send.at[k, 1], recv_sem=res_recv.at[origin, row],
            device_id={"tile": t + step * right, "freq": h}, device_id_type=MESH)

    def unit(left, i, right, h, n):
        k = PAIR[left, right]
        value = block(left, i, right, h)
        outbox[k, n] = value.astype(jnp.bfloat16)
        plain_send(left, i, right, h, n).start()
        if right == 0:
            @pl.when(h == f)
            def _():
                own[left, :, parts(i)] = value.T

            @pl.when(h != f)
            def _():
                turned[k, n] = value.T.astype(jnp.bfloat16)
                turned_send(left, i, right, h, n).start()
        else:
            turned[k, n] = value.T.astype(jnp.bfloat16)
            turned_send(left, i, right, h, n).start()

    def self_copy():
        return pltpu.make_async_remote_copy(
            src_ref=self_out, dst_ref=self_in, send_sem=self_send, recv_sem=self_recv,
            device_id={"freq": 1 - f}, device_id_type=MESH)

    for j in range(2):
        for which in range(2):
            own_copy(which, j).wait()

    @pl.loop(0, 4)
    def _(i):
        build_left(0, i)

    for target, dest in ((1 - f, self_out), (f, own.at[0])):
        @pl.loop(0, 4)
        def _(m):
            dest[parts(m // 2), columns(m % 2)] = block(0, 2 * target + m // 2, 0, m % 2)

        if dest is self_out:
            self_copy().start()

    @pl.loop(0, 4)
    def _(i):
        @pl.when(heavy)
        def _():
            for which in range(2):
                data_copy(which, i, 1).wait_recv()
            build_left(1, i)

            @pl.loop(0, 2)
            def _(h):
                unit(1, i, 0, h, 2 * i + h)

        @pl.when(has_far)
        def _():
            for which in range(2):
                data_copy(which, i, 2).wait_recv()
            build_left(2, i)

            @pl.loop(0, 2)
            def _(h):
                unit(2, i, 0, h, 2 * i + h)

        @pl.when(heavy & has_far)
        def _():
            @pl.loop(0, jnp.where(i == 1, 2, jnp.where(i == 0, 0, 2 * i - 3)))
            def _(m):
                n = jnp.where(i == 1, 2 * m, i + 2 + m)
                unit(2, n // 2, 1, n % 2, n)

            @pl.when(i >= 2)
            def _():
                unit(1, i, 2, 0, 2 * i - 3)

    self_copy().wait_recv()
    own[0] = own[0] + self_in[...]
    keep_copy = pltpu.make_async_copy(own, kept, kept_sem)
    keep_copy.start()

    def wait_inbox(origin, row):
        pltpu.make_async_remote_copy(
            src_ref=inbox.at[origin, row], dst_ref=inbox.at[origin, row],
            send_sem=res_send.at[0, 0], recv_sem=res_recv.at[origin, row],
            device_id={"freq": 1 - f}, device_id_type=MESH).wait_recv()

    for delta, row in ROW.items():
        @pl.when((r + delta >= 0) & (r + delta < tiles))
        def _():
            wait_inbox(1, ROW[-delta])
            if delta == 1:
                pl.when(jnp.logical_not(heavy))(lambda: wait_inbox(0, row))
            elif delta < 0:
                wait_inbox(0, row)

    keep_copy.wait()
    self_copy().wait_send()
    for i in range(4):
        for which in range(2):
            @pl.when(jnp.logical_not(heavy))
            def _():
                data_copy(which, i, 1).wait_send()

            @pl.when(r >= 2)
            def _():
                data_copy(which, i, 2).wait_send()

    def wait_sent(box, sem):
        pltpu.make_async_remote_copy(
            src_ref=box, dst_ref=box, send_sem=sem, recv_sem=res_recv.at[0, 0],
            device_id={"freq": 1 - f}, device_id_type=MESH).wait_send()

    for k, made in enumerate((heavy, has_far, heavy & has_far)):
        @pl.when(made)
        def _():
            wait_sent(outbox.at[k], res_send.at[k, 0])
            wait_sent(turned.at[k] if k == 2 else turned.at[k, 0:4], res_send.at[k, 1])


def join_kernel(tiles, radius, inbox_ref, kept_ref, band_ref, live_ref, out_ref, inbox, kept, out, inbox_sem, kept_sem, out_sem):
    t, f, step, r, heavy = place(tiles)
    _, half, points = kept.shape

    def inbox_copy(origin, row):
        return pltpu.make_async_copy(inbox_ref.at[origin, row], inbox.at[origin, row], inbox_sem.at[origin, row])

    def kept_copy(k):
        return pltpu.make_async_copy(kept_ref.at[k], kept.at[k], kept_sem.at[k])

    def out_copy(slot):
        return pltpu.make_async_copy(out.at[slot], out_ref.at[slot], out_sem.at[slot])

    order = (0, 2, 1, -1, -2)
    for delta in order:
        if delta >= 0:
            kept_copy(delta).start()
        if delta != 0:
            inbox_copy(1, ROW[-delta]).start()
            if delta < 2:
                inbox_copy(0, ROW[delta]).start()
    rows = lax.broadcasted_iota(jnp.int32, (half, points), 0) + f * half
    cols = lax.broadcasted_iota(jnp.int32, (half, points), 1)
    row_live = rows < live_ref[t]
    for delta in order:
        near = t + step * delta
        slot = radius + step * delta
        exists = (r + delta >= 0) & (r + delta < tiles)
        if delta >= 0:
            kept_copy(delta).wait()
        if delta != 0:
            inbox_copy(1, ROW[-delta]).wait()
            if delta < 2:
                inbox_copy(0, ROW[delta]).wait()

        def emit(read, near=near, slot=slot):
            keep = row_live & (cols < live_ref[near]) & (band_ref[t, slot] > 0)
            out[slot] = jnp.where(keep, read(), 0.0)

        def kept_sum(delta=delta):
            if delta == 0:
                return kept[0]
            return kept[delta] + inbox[1, ROW[-delta]].astype(jnp.float32)

        def inbox_sum(delta=delta):
            return inbox[0, ROW[delta]].astype(jnp.float32) + inbox[1, ROW[-delta]].astype(jnp.float32)

        if delta in (0, 2):
            pl.when(exists)(functools.partial(emit, kept_sum))
        elif delta == 1:
            pl.when(exists & heavy)(functools.partial(emit, kept_sum))
            pl.when(exists & jnp.logical_not(heavy))(functools.partial(emit, inbox_sum))
        else:
            pl.when(exists)(functools.partial(emit, inbox_sum))

        @pl.when(jnp.logical_not(exists))
        def _():
            out[slot] = jnp.zeros((half, points), jnp.float32)

        out_copy(slot).start()
    for slot in range(2 * radius + 1):
        out_copy(slot).wait()


def per_device(green_recv, green_shot, band_mask, live_counts, freq_bins):
    tiles = lax.axis_size("tile")
    points = green_recv.shape[3]
    slots = band_mask.shape[1]
    half = points // 2
    depth_r = 2 * green_recv.shape[2]
    depth_s = 2 * green_shot.shape[2]
    bf16, f32 = jnp.bfloat16, jnp.float32
    dma = pltpu.SemaphoreType.DMA
    smem = pl.BlockSpec(memory_space=pltpu.SMEM)
    anywhere = pl.BlockSpec(memory_space=pl.ANY)
    inbox, kept = pl.pallas_call(
        functools.partial(band_kernel, tiles),
        out_shape=(
            jax.ShapeDtypeStruct((2, 4, half, points), bf16),
            jax.ShapeDtypeStruct((3, half, points), f32),
        ),
        in_specs=[anywhere, anywhere, smem],
        out_specs=(anywhere, anywhere),
        scratch_shapes=[
            pltpu.VMEM((3, 2, depth_r, half), bf16),
            pltpu.VMEM((3, 2, depth_s, half), bf16),
            pltpu.VMEM((3, 4, half, depth_r), bf16),
            pltpu.VMEM((3, 4, half, depth_s), bf16),
            pltpu.VMEM((3, half, points), f32),
            pltpu.VMEM((half, points), f32),
            pltpu.VMEM((half, points), f32),
            pltpu.VMEM((3, 8, half // 2, half), bf16),
            pltpu.VMEM((3, 8, half, half // 2), bf16),
            dma((2, 2)),
            dma,
            dma((2, 4, 2)),
            dma((2, 4, 2)),
            dma((3, 2)),
            dma((2, 4)),
            dma,
            dma,
        ],
        compiler_params=pltpu.CompilerParams(
            collective_id=0, has_side_effects=True, vmem_limit_bytes=VMEM_MIB * 1024 * 1024),
    )(green_recv.reshape(depth_r, points), green_shot.reshape(depth_s, points), freq_bins)
    band = pl.pallas_call(
        functools.partial(join_kernel, tiles, slots // 2),
        out_shape=jax.ShapeDtypeStruct((slots, half, points), f32),
        in_specs=[anywhere, anywhere, smem, smem],
        out_specs=anywhere,
        scratch_shapes=[
            pltpu.VMEM((2, 4, half, points), bf16),
            pltpu.VMEM((3, half, points), f32),
            pltpu.VMEM((slots, half, points), f32),
            dma((2, 4)),
            dma((3,)),
            dma((slots,)),
        ],
        compiler_params=pltpu.CompilerParams(vmem_limit_bytes=VMEM_MIB * 1024 * 1024),
    )(inbox, kept, band_mask, live_counts)
    return jnp.transpose(band, (1, 0, 2))


def solution(mesh):
    return jax.shard_map(
        per_device,
        mesh=mesh,
        in_specs=(
            P(("grp", "freq"), None, None, "tile"),
            P(("grp", "freq"), None, None, "tile"),
            P("grp", None),
            P("grp"),
            P(("grp", "freq")),
        ),
        out_specs=P(("grp", "tile", "freq"), None, None),
        check_vma=False,
    )
```

```python
import functools

import jax
import jax.numpy as jnp
from jax import lax
from jax.experimental import pallas as pl
from jax.experimental.pallas import tpu as pltpu
from jax.sharding import PartitionSpec as P

BINS = 512
VMEM_MIB = 60
MESH = pl.DeviceIdType.MESH
PAIR = {(1, 0): 0, (2, 0): 1, (2, 1): 2, (1, 2): 2}
ROW = {1: 0, 2: 1, -1: 2, -2: 3}


def place(tiles):
    t = lax.axis_index("tile")
    f = lax.axis_index("freq")
    step = 1 - 2 * f
    r = f * (tiles - 1) + step * t
    return t, f, step, r, lax.rem(r, 2) == 0


def band_kernel(tiles, recv_ref, shot_ref, bins_ref, inbox, kept,
                far_r, far_s, left_r, left_s, own, self_out, self_in, outbox, turned,
                own_sem, kept_sem, data_send, data_recv, res_send, res_recv, self_send, self_recv):
    t, f, step, r, heavy = place(tiles)
    depth_r, points = recv_ref.shape
    depth_s = shot_ref.shape[0]
    half = points // 2
    part = half // 2
    has_far = r + 2 < tiles
    weight_root = bins_ref[0].astype(jnp.float32) / BINS
    weight = (weight_root * weight_root) * (weight_root * weight_root)

    def columns(j):
        return pl.ds(pl.multiple_of(j * half, half), half)

    def parts(i):
        return pl.ds(pl.multiple_of(i * part, part), part)

    def own_copy(which, j):
        src, dst = ((recv_ref, far_r), (shot_ref, far_s))[which]
        return pltpu.make_async_copy(src.at[:, columns(j)], dst.at[0, j], own_sem.at[which, j])

    def data_copy(which, i, distance):
        src, dst = ((recv_ref, far_r), (shot_ref, far_s))[which]
        return pltpu.make_async_remote_copy(
            src_ref=src.at[:, parts(i)], dst_ref=dst.at[distance, i // 2, :, parts(i % 2)],
            send_sem=data_send.at[which, i, distance - 1], recv_sem=data_recv.at[which, i, distance - 1],
            device_id={"tile": t - step * distance}, device_id_type=MESH)

    barrier = pltpu.get_barrier_semaphore()
    for distance in range(-2, 3):
        near = t + distance
        for turn in range(2):
            if distance == 0 and turn == 0:
                continue
            other = f if turn == 0 else 1 - f

            @pl.when((near >= 0) & (near < tiles))
            def _():
                pl.semaphore_signal(barrier, inc=1, device_id={"tile": near, "freq": other}, device_id_type=MESH)
    reached = jnp.minimum(t, 2) + jnp.minimum(tiles - 1 - t, 2)
    for j in range(2):
        for which in range(2):
            own_copy(which, j).start()

    pl.semaphore_wait(barrier, 2 * reached + 1)

    for i in range(4):
        for which in range(2):
            @pl.when(jnp.logical_not(heavy))
            def _():
                data_copy(which, i, 1).start()

            @pl.when(r >= 2)
            def _():
                data_copy(which, i, 2).start()

    def build_left(slot, i):
        for src, dst, depth in ((far_r, left_r, depth_r // 2), (far_s, left_s, depth_s // 2)):
            re = src[slot, i // 2, 0:depth, parts(i % 2)].T
            im = src[slot, i // 2, depth:2 * depth, parts(i % 2)].T
            dst[slot, i, 0:part, 0:depth] = re
            dst[slot, i, 0:part, depth:2 * depth] = im
            dst[slot, i, part:half, 0:depth] = im
            dst[slot, i, part:half, depth:2 * depth] = -re

    def block(left, i, right, h):
        rr = jnp.dot(left_r[left, i], far_r[right, h], preferred_element_type=jnp.float32)
        ss = jnp.dot(left_s[left, i], far_s[right, h], preferred_element_type=jnp.float32)
        return (rr[:part] * ss[:part] - rr[part:] * ss[part:]) * weight

    def origin_at(h):
        return jnp.where(h == f, 0, 1)

    def plain_send(left, i, right, h, n):
        k, origin, row = PAIR[left, right], origin_at(i // 2), ROW[right - left]
        return pltpu.make_async_remote_copy(
            src_ref=outbox.at[k, n], dst_ref=inbox.at[origin, row, parts(i % 2), columns(h)],
            send_sem=res_send.at[k, 0], recv_sem=res_recv.at[origin, row],
            device_id={"tile": t + step * left, "freq": i // 2}, device_id_type=MESH)

    def turned_send(left, i, right, h, n):
        k, origin, row = PAIR[left, right], origin_at(h), ROW[left - right]
        return pltpu.make_async_remote_copy(
            src_ref=turned.at[k, n], dst_ref=inbox.at[origin, row, :, parts(i)],
            send_sem=res_send.at[k, 1], recv_sem=res_recv.at[origin, row],
            device_id={"tile": t + step * right, "freq": h}, device_id_type=MESH)

    def unit(left, i, right, h, n):
        k = PAIR[left, right]
        value = block(left, i, right, h)
        outbox[k, n] = value.astype(jnp.bfloat16)
        plain_send(left, i, right, h, n).start()
        if right == 0:
            @pl.when(h == f)
            def _():
                own[left, :, parts(i)] = value.T

            @pl.when(h != f)
            def _():
                turned[k, n] = value.T.astype(jnp.bfloat16)
                turned_send(left, i, right, h, n).start()
        else:
            turned[k, n] = value.T.astype(jnp.bfloat16)
            turned_send(left, i, right, h, n).start()

    def self_copy():
        return pltpu.make_async_remote_copy(
            src_ref=self_out, dst_ref=self_in, send_sem=self_send, recv_sem=self_recv,
            device_id={"freq": 1 - f}, device_id_type=MESH)

    for j in range(2):
        for which in range(2):
            own_copy(which, j).wait()

    @pl.loop(0, 4)
    def _(i):
        build_left(0, i)

    for target, dest in ((1 - f, self_out), (f, own.at[0])):
        @pl.loop(0, 4)
        def _(m):
            dest[parts(m // 2), columns(m % 2)] = block(0, 2 * target + m // 2, 0, m % 2)

        if dest is self_out:
            self_copy().start()

    @pl.loop(0, 4)
    def _(i):
        @pl.when(heavy)
        def _():
            for which in range(2):
                data_copy(which, i, 1).wait_recv()
            build_left(1, i)

            @pl.loop(0, 2)
            def _(h):
                unit(1, i, 0, h, 2 * i + h)

        @pl.when(heavy & has_far & (i >= 2))
        def _():
            unit(1, i, 2, 0, 2 * i - 3)

        @pl.when(has_far)
        def _():
            for which in range(2):
                data_copy(which, i, 2).wait_recv()
            build_left(2, i)

            @pl.loop(0, 2)
            def _(h):
                unit(2, i, 0, h, 2 * i + h)

        @pl.when(heavy & has_far)
        def _():
            @pl.loop(0, jnp.where(i == 1, 2, jnp.where(i == 0, 0, 2 * i - 3)))
            def _(m):
                n = jnp.where(i == 1, 2 * m, i + 2 + m)
                unit(2, n // 2, 1, n % 2, n)

    self_copy().wait_recv()
    own[0] = own[0] + self_in[...]
    keep_copy = pltpu.make_async_copy(own, kept, kept_sem)
    keep_copy.start()

    def wait_inbox(origin, row):
        pltpu.make_async_remote_copy(
            src_ref=inbox.at[origin, row], dst_ref=inbox.at[origin, row],
            send_sem=res_send.at[0, 0], recv_sem=res_recv.at[origin, row],
            device_id={"freq": 1 - f}, device_id_type=MESH).wait_recv()

    for delta, row in ROW.items():
        @pl.when((r + delta >= 0) & (r + delta < tiles))
        def _():
            wait_inbox(1, ROW[-delta])
            if delta == 1:
                pl.when(jnp.logical_not(heavy))(lambda: wait_inbox(0, row))
            elif delta < 0:
                wait_inbox(0, row)

    keep_copy.wait()
    self_copy().wait_send()
    for i in range(4):
        for which in range(2):
            @pl.when(jnp.logical_not(heavy))
            def _():
                data_copy(which, i, 1).wait_send()

            @pl.when(r >= 2)
            def _():
                data_copy(which, i, 2).wait_send()

    def wait_sent(box, sem):
        pltpu.make_async_remote_copy(
            src_ref=box, dst_ref=box, send_sem=sem, recv_sem=res_recv.at[0, 0],
            device_id={"freq": 1 - f}, device_id_type=MESH).wait_send()

    for k, made in enumerate((heavy, has_far, heavy & has_far)):
        @pl.when(made)
        def _():
            wait_sent(outbox.at[k], res_send.at[k, 0])
            wait_sent(turned.at[k] if k == 2 else turned.at[k, 0:4], res_send.at[k, 1])


def join_kernel(tiles, radius, inbox_ref, kept_ref, band_ref, live_ref, out_ref, inbox, kept, out, inbox_sem, kept_sem, out_sem):
    t, f, step, r, heavy = place(tiles)
    _, half, points = kept.shape

    def inbox_copy(origin, row):
        return pltpu.make_async_copy(inbox_ref.at[origin, row], inbox.at[origin, row], inbox_sem.at[origin, row])

    def kept_copy(k):
        return pltpu.make_async_copy(kept_ref.at[k], kept.at[k], kept_sem.at[k])

    def out_copy(slot):
        return pltpu.make_async_copy(out.at[slot], out_ref.at[slot], out_sem.at[slot])

    order = (0, 2, 1, -1, -2)
    for delta in order:
        if delta == 1:
            pl.when(heavy)(kept_copy(1).start)
            pl.when(jnp.logical_not(heavy))(inbox_copy(0, ROW[1]).start)
        elif delta >= 0:
            kept_copy(delta).start()
        else:
            inbox_copy(0, ROW[delta]).start()
        if delta != 0:
            inbox_copy(1, ROW[-delta]).start()
    rows = lax.broadcasted_iota(jnp.int32, (half, points), 0) + f * half
    cols = lax.broadcasted_iota(jnp.int32, (half, points), 1)
    row_live = rows < live_ref[t]
    for delta in order:
        near = t + step * delta
        slot = radius + step * delta
        exists = (r + delta >= 0) & (r + delta < tiles)
        if delta == 1:
            pl.when(heavy)(kept_copy(1).wait)
            pl.when(jnp.logical_not(heavy))(inbox_copy(0, ROW[1]).wait)
        elif delta >= 0:
            kept_copy(delta).wait()
        else:
            inbox_copy(0, ROW[delta]).wait()
        if delta != 0:
            inbox_copy(1, ROW[-delta]).wait()

        def emit(read, near=near, slot=slot):
            keep = row_live & (cols < live_ref[near]) & (band_ref[t, slot] > 0)
            out[slot] = jnp.where(keep, read(), 0.0)

        def kept_sum(delta=delta):
            if delta == 0:
                return kept[0]
            return kept[delta] + inbox[1, ROW[-delta]].astype(jnp.float32)

        def inbox_sum(delta=delta):
            return inbox[0, ROW[delta]].astype(jnp.float32) + inbox[1, ROW[-delta]].astype(jnp.float32)

        if delta in (0, 2):
            pl.when(exists)(functools.partial(emit, kept_sum))
        elif delta == 1:
            pl.when(exists & heavy)(functools.partial(emit, kept_sum))
            pl.when(exists & jnp.logical_not(heavy))(functools.partial(emit, inbox_sum))
        else:
            pl.when(exists)(functools.partial(emit, inbox_sum))

        @pl.when(jnp.logical_not(exists))
        def _():
            out[slot] = jnp.zeros((half, points), jnp.float32)

        out_copy(slot).start()
    for slot in range(2 * radius + 1):
        out_copy(slot).wait()


def per_device(green_recv, green_shot, band_mask, live_counts, freq_bins):
    tiles = lax.axis_size("tile")
    points = green_recv.shape[3]
    slots = band_mask.shape[1]
    half = points // 2
    depth_r = 2 * green_recv.shape[2]
    depth_s = 2 * green_shot.shape[2]
    bf16, f32 = jnp.bfloat16, jnp.float32
    dma = pltpu.SemaphoreType.DMA
    smem = pl.BlockSpec(memory_space=pltpu.SMEM)
    anywhere = pl.BlockSpec(memory_space=pl.ANY)
    inbox, kept = pl.pallas_call(
        functools.partial(band_kernel, tiles),
        out_shape=(
            jax.ShapeDtypeStruct((2, 4, half, points), bf16),
            jax.ShapeDtypeStruct((3, half, points), f32),
        ),
        in_specs=[anywhere, anywhere, smem],
        out_specs=(anywhere, anywhere),
        scratch_shapes=[
            pltpu.VMEM((3, 2, depth_r, half), bf16),
            pltpu.VMEM((3, 2, depth_s, half), bf16),
            pltpu.VMEM((3, 4, half, depth_r), bf16),
            pltpu.VMEM((3, 4, half, depth_s), bf16),
            pltpu.VMEM((3, half, points), f32),
            pltpu.VMEM((half, points), f32),
            pltpu.VMEM((half, points), f32),
            pltpu.VMEM((3, 8, half // 2, half), bf16),
            pltpu.VMEM((3, 8, half, half // 2), bf16),
            dma((2, 2)),
            dma,
            dma((2, 4, 2)),
            dma((2, 4, 2)),
            dma((3, 2)),
            dma((2, 4)),
            dma,
            dma,
        ],
        compiler_params=pltpu.CompilerParams(
            collective_id=0, has_side_effects=True, vmem_limit_bytes=VMEM_MIB * 1024 * 1024),
    )(green_recv.reshape(depth_r, points), green_shot.reshape(depth_s, points), freq_bins)
    band = pl.pallas_call(
        functools.partial(join_kernel, tiles, slots // 2),
        out_shape=jax.ShapeDtypeStruct((slots, half, points), f32),
        in_specs=[anywhere, anywhere, smem, smem],
        out_specs=anywhere,
        scratch_shapes=[
            pltpu.VMEM((2, 4, half, points), bf16),
            pltpu.VMEM((3, half, points), f32),
            pltpu.VMEM((slots, half, points), f32),
            dma((2, 4)),
            dma((3,)),
            dma((slots,)),
        ],
        compiler_params=pltpu.CompilerParams(vmem_limit_bytes=VMEM_MIB * 1024 * 1024),
    )(inbox, kept, band_mask, live_counts)
    return jnp.transpose(band, (1, 0, 2))


def solution(mesh):
    return jax.shard_map(
        per_device,
        mesh=mesh,
        in_specs=(
            P(("grp", "freq"), None, None, "tile"),
            P(("grp", "freq"), None, None, "tile"),
            P("grp", None),
            P("grp"),
            P(("grp", "freq")),
        ),
        out_specs=P(("grp", "tile", "freq"), None, None),
        check_vma=False,
    )
```
